32 devices in a mesh: parts: 2 (over y), wide: 4 (over z), narrow: 2 (over x), pair: 2 (over core).
Axes of the slice: x: 2, y: 2, z: 4, core: 2. Of those that a mesh axis runs over, the one named last changes fastest.
Arguments:
- low_sino: bfloat16 [8, 24, 32, 512], P(('parts', 'wide'), None, None, ('narrow', 'pair')), parts along dimension 0, may hold values from -6 to 6
- angle_weight: bfloat16 [4, 24, 24], replicated, may hold values from -1.25 to 1.25
- angle_bias: float32 [24], replicated, may hold values from -3 to 3
- column_weight: bfloat16 [4, 24, 24], replicated, may hold values from -0.875 to 0.875
- column_bias: float32 [24], replicated, may hold values from -3 to 3
- head_weight: float32 [24], replicated, may hold values from -1.25 to 1.25
- sparse_views: int32 [4, 16], P(('parts', 'narrow')), parts along dimension 0, may hold values from 0 to 7
- measured: float32 [32, 16, 512], P('parts', 'wide', ('narrow', 'pair')), parts along dimension 0, may hold values from -6 to 6
- row_weights: float32 [512, 512], P(('narrow', 'pair')), may hold values from -0.25 to 0.25
Outputs:
- predicted: float32 [16, 16, 512], P('parts', 'wide', ('narrow', 'pair')), parts along dimension 0
- adjoint: float32 [32, 16, 512], P('parts', 'wide', ('narrow', 'pair')), parts along dimension 0
The draws below stay inside these ranges and needn't reach their ends.
There are 2 independent parts, one for each index of `parts`. The reference program is written for one: setup_inputs(seed, part) draws one part's arguments, and reference() takes and returns one part's arrays. A program takes and returns all parts, laid end to end along the dimension named above; an argument that names none is the same for every part. Nothing has to cross between parts.
All inputs are finite; a program needn't handle non-finite values.
Results may differ from the reference program's by a relative error of at most 0.0034.
Values may be sent and summed in bfloat16 or wider, within the bound.
A program may use at most 64 MiB of HBM per device.

```python
import jax
import jax.numpy as jnp
from jax import lax

C = 24
ROW_DEV = 128
K = 16
V_IN = 4
V_OUT = 8
W = 32
WOUT = 16
ROWS = 512
BANDS = 2


def touch_ends(result, key, least, top_value):
    extent = result.shape
    spot = [jax.random.randint(jax.random.fold_in(key, axis), (), 0, extent[axis]) for axis in range(len(extent))]
    result = result.at[tuple(spot)].set(least)
    longest = extent.index(max(extent))
    spot[longest] = (spot[longest] + 1) % extent[longest]
    return result.at[tuple(spot)].set(top_value)


def level_of(own_key, extent, cuts, low, largest):
    def one(position, shards_of):
        heights = jax.random.uniform(jax.random.fold_in(jax.random.fold_in(own_key, 6), position), (shards_of,), jnp.float32, low / len(cuts), largest / len(cuts))
        return jnp.repeat(jnp.exp(heights), extent[position] // shards_of).reshape((-1,) + (1,) * (len(extent) - position - 1))

    factor_of = one(*cuts[0])
    for cut in cuts[1:]:
        factor_of = factor_of * one(*cut)
    return factor_of


def noise(rng, dims, spread, reach, cuts=(), kind=jnp.bfloat16):
    result = spread * jax.random.normal(rng, dims, jnp.float32)
    if cuts:
        result = result * level_of(rng, dims, cuts, -0.22, 0.18)
    return jnp.clip(result, -reach, reach).astype(kind)


def setup_inputs(seed: int = 0, part: int = 0) -> dict:
    splits = jax.random.split(jax.random.key(seed), 10)
    part_keys = jax.random.split(jax.random.fold_in(splits[9], part), 10)
    low_sino = noise(part_keys[0], (V_IN, C, W, ROWS), 1.0, 6.0, ((0, 4), (3, 4)))
    angle_weight = noise(splits[1], (4, C, C), C ** -0.5, 1.25)
    angle_bias = noise(splits[2], (C,), 0.5, 3.0, (), jnp.float32)
    column_weight = noise(splits[3], (4, C, C), (2 * C) ** -0.5, 0.875)
    column_bias = noise(splits[4], (C,), 0.5, 3.0, (), jnp.float32)
    head_weight = noise(splits[5], (C,), C ** -0.5, 1.25, (), jnp.float32)
    sparse_views = touch_ends(jax.random.randint(part_keys[6], (BANDS, K), 0, V_OUT), jax.random.fold_in(part_keys[6], 1), 0, V_OUT - 1).astype(jnp.int32)
    measured = noise(part_keys[7], (K, WOUT, ROWS), 1.0, 6.0, ((1, 4), (2, 4)), jnp.float32)
    row_weights = noise(splits[8], (ROWS, ROWS), ROWS ** -0.5, 0.25, ((0, 4),), jnp.float32)
    return {"low_sino": low_sino, "angle_weight": angle_weight, "angle_bias": angle_bias, "column_weight": column_weight, "column_bias": column_bias, "head_weight": head_weight, "sparse_views": sparse_views, "measured": measured, "row_weights": row_weights}


def leaky_relu(values):
    return jnp.where(values > 0, values, 0.1 * values)


def channel_mix(inputs, weight):
    return jnp.einsum('vcwr,cd->vdwr', inputs.astype(jnp.float32), weight.astype(jnp.float32))


def upsample(current, weight, bias_values):
    previous = jnp.roll(current, 1, axis=0)
    even_views = channel_mix(current, weight[0]) + channel_mix(previous, weight[2])
    odd_views = channel_mix(current, weight[1]) + channel_mix(previous, weight[3])
    stacked = jnp.stack([even_views, odd_views], axis=1) + bias_values[None, None, :, None, None]
    return leaky_relu(stacked).reshape(2 * current.shape[0], current.shape[1], current.shape[2], current.shape[3]).astype(jnp.bfloat16)


def detector_layer(upsampled, weight, bias_values, head_weight):
    padded = jnp.pad(upsampled, ((0, 0), (0, 0), (1, 1), (0, 0)))
    col_count = upsampled.shape[2]
    summed = channel_mix(padded[:, :, 0:col_count:2], weight[0])
    for tap_index in range(1, 4):
        summed = summed + channel_mix(padded[:, :, tap_index:tap_index + col_count:2], weight[tap_index])
    hidden = leaky_relu(summed + bias_values[None, :, None, None])
    return jnp.sum(hidden * head_weight[None, :, None, None], axis=1)


def reference(low_sino, angle_weight, angle_bias, column_weight, column_bias, head_weight, sparse_views, measured, row_weights):
    def one_block(block_index):
        row_block = lax.dynamic_slice_in_dim(low_sino, block_index * ROW_DEV, ROW_DEV, 3)
        upsampled = upsample(row_block, angle_weight, angle_bias)
        return detector_layer(upsampled, column_weight, column_bias, head_weight)

    blocks = lax.map(one_block, jnp.arange(ROWS // ROW_DEV, dtype=jnp.int32))
    predicted = jnp.transpose(blocks, (1, 2, 0, 3)).reshape(V_OUT, WOUT, ROWS)
    banded = predicted.reshape(V_OUT, WOUT, BANDS, ROWS // BANDS)
    picked = jnp.stack([jnp.take(banded[:, :, band_index], sparse_views[band_index], axis=0) for band_index in range(BANDS)], axis=2)
    residual_slab = picked.reshape(K, WOUT, ROWS) - measured
    adjoint = jnp.einsum('kjr,zr->kjz', residual_slab, row_weights, precision=lax.Precision.HIGHEST)
    return (predicted, adjoint)
```

```python
import functools

import jax
import jax.numpy as jnp
from jax import lax
from jax.experimental import pallas as pl
from jax.experimental.pallas import tpu as pltpu
from jax.sharding import PartitionSpec as P

F32 = jnp.float32
BF16 = jnp.bfloat16


def indices(rows, cols, axis):
    return lax.broadcasted_iota(jnp.int32, (rows, cols), axis).astype(F32)


def div(values, divisor):
    return jnp.floor((values + 0.5) * (1.0 / divisor))


def one_hot(hit):
    return jnp.where(hit, 1.0, 0.0).astype(F32)


def leaky(values):
    return jnp.maximum(values, 0.1 * values)


def nt_dot(left, right, precision=None):
    return lax.dot_general(
        left, right, (((1,), (1,)), ((), ())), precision=precision, preferred_element_type=F32
    )


def angle_matrix(weight, chans):
    size = 4 * chans
    row, col = indices(size, size, 0), indices(size, size, 1)
    row_block, col_block = div(row, chans), div(col, chans)
    spread_row = indices(size, chans, 0)
    left = one_hot(spread_row - chans * div(spread_row, chans) == indices(size, chans, 1)).astype(BF16)
    spread_col = indices(chans, size, 1)
    right = one_hot(spread_col - chans * div(spread_col, chans) == indices(chans, size, 0)).astype(BF16)
    parity, side = div(row_block, 2), div(col_block, 2)
    same = (row_block - 2 * parity) == (col_block - 2 * side)
    total = jnp.zeros((size, size), F32)
    for tap in range(4):
        spread = nt_dot(left, weight[tap]).astype(BF16)
        spread = jnp.dot(spread, right, preferred_element_type=F32)
        total = jnp.where(same & (parity + 2 * side == tap), spread, total)
    return total.astype(BF16)


def column_matrix(weight, chans, outs, first, last):
    rows, cols = chans * outs, 2 * (outs + 1) * chans
    row, col = indices(rows, cols, 0), indices(rows, cols, 1)
    out_col = row - outs * div(row, outs)
    in_col = div(col, chans)
    left = one_hot(div(indices(rows, chans, 0), outs) == indices(rows, chans, 1)).astype(BF16)
    spread_col = indices(chans, cols, 1)
    right = one_hot(spread_col - chans * div(spread_col, chans) == indices(chans, cols, 0)).astype(BF16)
    total = jnp.zeros((rows, cols), F32)
    for tap in range(4):
        spread = nt_dot(left, weight[tap]).astype(BF16)
        spread = jnp.dot(spread, right, preferred_element_type=F32)
        total = jnp.where(in_col - 2 * out_col == tap, spread, total)
    outside = ((in_col == 0) & first) | ((in_col == 2 * outs + 1) & last)
    return jnp.where(outside, 0.0, total).astype(BF16)


def kernel(
    wide, narrow, pair, outs,
    x_hbm, aw_hbm, ab_hbm, cw_hbm, cb_hbm, hw_hbm, sv_hbm, meas_hbm, rw_hbm,
    pred_hbm, adj_hbm,
    x_in, x_cols, x_all, aw, ab, cw, cb, hw, sv_all, sv_s, meas_all, rows_m, rw,
    pred_all, pred_out, adj_out, picks,
    in_sem, sv_sem, out_sem, x_send, x_recv, m_send, m_recv, s_send, s_recv, p_send, p_recv,
):
    me = lax.axis_index("wide")
    my_n, my_p = lax.axis_index("narrow"), lax.axis_index("pair")
    group = narrow * pair
    my_g = my_n * pair + my_p
    chans, lanes = x_in.shape[1], x_in.shape[3]
    views = x_in.shape[0]
    pairs = outs + 1
    all_views = wide * views
    keep = meas_all.shape[1]

    def row_peer(step):
        other = lax.rem(my_g + step, group)
        return other, {"narrow": lax.div(other, pair), "pair": lax.rem(other, pair)}

    barrier = pltpu.get_barrier_semaphore()
    for step in range(1, wide):
        pl.semaphore_signal(
            barrier, inc=1, device_id={"wide": lax.rem(me + step, wide)}, device_id_type=pl.DeviceIdType.MESH
        )
    for step in range(1, group):
        pl.semaphore_signal(
            barrier, inc=1, device_id=row_peer(step)[1], device_id_type=pl.DeviceIdType.MESH
        )

    loads = [
        pltpu.make_async_copy(source, target, in_sem.at[spot])
        for spot, (source, target) in enumerate(
            [
                (x_hbm, x_in), (aw_hbm, aw), (ab_hbm, ab), (cw_hbm, cw), (cb_hbm, cb), (hw_hbm, hw),
                (rw_hbm, rw), (meas_hbm, meas_all.at[my_g]), (sv_hbm, sv_all.at[my_n]),
            ]
        )
    ]
    for load in loads:
        load.start()

    loads[0].wait()
    blank = jnp.zeros((1, chans, lanes), F32)
    for view in range(views):
        turned = jnp.swapaxes(x_in[view].astype(F32), 0, 1)
        padded = jnp.concatenate([blank, turned, blank], axis=0)
        x_cols[view] = padded.reshape(x_cols.shape[1], 2 * chans, lanes).astype(BF16)

    pl.semaphore_wait(barrier, wide - 1 + group - 1)

    order = sorted(range(1, wide), key=lambda step: abs(step - wide // 2))
    sends = []
    for step in order:
        target = lax.rem(me + step, wide)
        sends.append(
            pltpu.make_async_remote_copy(
                src_ref=x_cols.at[:, pl.ds(outs * target, pairs)],
                dst_ref=x_all.at[me],
                send_sem=x_send.at[step],
                recv_sem=x_recv.at[me],
                device_id={"wide": target},
                device_id_type=pl.DeviceIdType.MESH,
            )
        )
        sends[-1].start()
    loads[7].wait()
    loads[8].wait()
    for step in range(1, group):
        other, where = row_peer(step)
        sends.append(
            pltpu.make_async_remote_copy(
                src_ref=meas_all.at[my_g],
                dst_ref=meas_all.at[my_g],
                send_sem=m_send.at[step],
                recv_sem=m_recv.at[my_g],
                device_id=where,
                device_id_type=pl.DeviceIdType.MESH,
            )
        )
        sends[-1].start()
    for step in range(1, narrow):
        sends.append(
            pltpu.make_async_remote_copy(
                src_ref=sv_all.at[my_n],
                dst_ref=sv_all.at[my_n],
                send_sem=s_send.at[step],
                recv_sem=s_recv.at[my_n],
                device_id={"narrow": lax.rem(my_n + step, narrow)},
                device_id_type=pl.DeviceIdType.MESH,
            )
        )
        sends[-1].start()
    x_all[me] = x_cols[:, pl.ds(outs * me, pairs)]

    for load in loads[1:7]:
        load.wait()
    angle = angle_matrix(aw, chans)
    column = column_matrix(cw, chans, outs, me == 0, me == wide - 1)
    pick_row = indices(4 * chans, chans, 0)
    angle_bias = jnp.sum(
        one_hot(pick_row - chans * div(pick_row, chans) == indices(4 * chans, chans, 1)) * ab[...],
        axis=1, keepdims=True,
    )
    head_hot = one_hot(div(indices(outs * chans, chans, 0), outs) == indices(outs * chans, chans, 1))
    column_bias = jnp.sum(head_hot * cb[...], axis=1, keepdims=True)
    head = jnp.sum(head_hot * hw[...], axis=1, keepdims=True)

    def wait_for(block, sem):
        pltpu.make_async_remote_copy(
            src_ref=block, dst_ref=block, send_sem=x_send.at[0], recv_sem=sem,
            device_id={"wide": me}, device_id_type=pl.DeviceIdType.MESH,
        ).wait_recv()

    for step in range(1, group):
        other = row_peer(step)[0]
        wait_for(meas_all.at[other], m_recv.at[other])
    for step in range(1, narrow):
        other = lax.rem(my_n + step, narrow)
        wait_for(sv_all.at[other], s_recv.at[other])
    fetch = pltpu.make_async_copy(sv_all, sv_s, sv_sem)
    fetch.start()
    for block in range(group):
        for spot in range(keep):
            rows_m[pl.ds(spot * outs, outs), pl.ds(block * lanes, lanes)] = meas_all[block, spot]
    measured = nt_dot(rows_m[...], rw[...], lax.Precision.HIGHEST)
    rows_m[:, : rw.shape[0]] = measured
    fetch.wait()

    fold = 8 // outs
    arrived = set()
    for step in range(wide):
        for near in (step, step + wide - 1):
            near %= wide
            if near and near not in arrived:
                source = lax.rem(me + near, wide)
                wait_for(x_all.at[source], x_recv.at[source])
                arrived.add(near)
        for view in range(views):
            now = lax.rem(me + step, wide) * views + view
            before = lax.rem(now + all_views - 1, all_views)
            current = x_all[lax.div(now, views), lax.rem(now, views)]
            previous = x_all[lax.div(before, views), lax.rem(before, views)]
            inputs = jnp.concatenate(
                [
                    jnp.concatenate([current[spot], previous[spot]], axis=0)
                    for spot in range(pairs)
                ],
                axis=1,
            )
            raised = jnp.dot(angle, inputs, preferred_element_type=F32)
            raised = leaky(raised + angle_bias).astype(BF16)
            stacked = jnp.concatenate(
                [
                    jnp.concatenate(
                        [
                            raised[parity * 2 * chans : (parity + 1) * 2 * chans, spot * lanes : (spot + 1) * lanes]
                            for spot in range(pairs)
                        ],
                        axis=0,
                    )
                    for parity in range(2)
                ],
                axis=1,
            )
            hidden = jnp.dot(column, stacked, preferred_element_type=F32)
            hidden = leaky(hidden + column_bias) * head
            summed = jnp.sum(hidden.reshape(chans // fold, 8, 2 * lanes), axis=0)
            even, odd = summed[:, :lanes], summed[:, lanes:]
            shift = outs
            while shift < 8:
                even = even + pltpu.roll(even, shift, axis=0)
                odd = odd + pltpu.roll(odd, shift, axis=0)
                shift *= 2
            row = lax.broadcasted_iota(jnp.int32, even.shape, 0)
            both = jnp.where(row < outs, even, odd)
            pred_all[my_g, now] = both
            pred_out[2 * now] = both[:outs]
            pred_out[2 * now + 1] = both[outs : 2 * outs]

    finals = []
    for step in range(1, group):
        other, where = row_peer(step)
        finals.append(
            pltpu.make_async_remote_copy(
                src_ref=pred_all.at[my_g],
                dst_ref=pred_all.at[my_g],
                send_sem=p_send.at[step],
                recv_sem=p_recv.at[my_g],
                device_id=where,
                device_id_type=pl.DeviceIdType.MESH,
            )
        )
        finals[-1].start()
    store = pltpu.make_async_copy(pred_out, pred_hbm, out_sem.at[0])
    store.start()
    for step in range(1, group):
        other = row_peer(step)[0]
        wait_for(pred_all.at[other], p_recv.at[other])

    for band in range(narrow):
        total = jnp.zeros((8 * all_views, rw.shape[0]), F32)
        for block in range(band * pair, (band + 1) * pair):
            total += nt_dot(
                pred_all[block].reshape(8 * all_views, lanes),
                rw[:, block * lanes : (block + 1) * lanes],
                lax.Precision.HIGHEST,
            )
        for view in range(all_views):
            picks[band, 2 * view] = total[8 * view : 8 * view + outs]
            picks[band, 2 * view + 1] = total[8 * view + outs : 8 * view + 2 * outs]
    for spot in range(keep):
        value = picks[0, sv_s[0, 0, spot]]
        for band in range(1, narrow):
            value = value + picks[band, sv_s[band, 0, spot]]
        adj_out[spot] = value - rows_m[pl.ds(spot * outs, outs), : rw.shape[0]]
    last = pltpu.make_async_copy(adj_out, adj_hbm, out_sem.at[1])
    last.start()
    for send in sends + finals:
        send.wait_send()
    store.wait()
    last.wait()


def local(
    wide, narrow, pair,
    low_sino, angle_weight, angle_bias, column_weight, column_bias, head_weight,
    sparse_views, measured, row_weights,
):
    views, chans, cols, lanes = low_sino.shape
    keep, outs, _ = measured.shape
    depth = row_weights.shape[0]
    group = narrow * pair
    all_views = wide * views
    any_space = pl.BlockSpec(memory_space=pl.ANY)
    dma = pltpu.SemaphoreType.DMA
    return pl.pallas_call(
        functools.partial(kernel, wide, narrow, pair, outs),
        out_shape=(
            jax.ShapeDtypeStruct((2 * all_views, outs, lanes), F32),
            jax.ShapeDtypeStruct((keep, outs, depth), F32),
        ),
        in_specs=[any_space] * 9,
        out_specs=(any_space, any_space),
        scratch_shapes=[
            pltpu.VMEM(low_sino.shape, BF16),
            pltpu.VMEM((views, cols // 2 + 1, 2 * chans, lanes), BF16),
            pltpu.VMEM((wide, views, outs + 1, 2 * chans, lanes), BF16),
            pltpu.VMEM(angle_weight.shape, BF16),
            pltpu.VMEM((1, chans), F32),
            pltpu.VMEM(column_weight.shape, BF16),
            pltpu.VMEM((1, chans), F32),
            pltpu.VMEM((1, chans), F32),
            pltpu.VMEM((narrow, 1, keep), jnp.int32),
            pltpu.SMEM((narrow, 1, keep), jnp.int32),
            pltpu.VMEM((group, keep, outs, lanes), F32),
            pltpu.VMEM((keep * outs, group * lanes), F32),
            pltpu.VMEM(row_weights.shape, F32),
            pltpu.VMEM((group, all_views, 8, lanes), F32),
            pltpu.VMEM((2 * all_views, outs, lanes), F32),
            pltpu.VMEM((keep, outs, depth), F32),
            pltpu.VMEM((narrow, 2 * all_views, outs, depth), F32),
            dma((9,)), dma, dma((2,)),
            dma((wide,)), dma((wide,)),
            dma((group,)), dma((group,)),
            dma((narrow,)), dma((narrow,)),
            dma((group,)), dma((group,)),
        ],
        compiler_params=pltpu.CompilerParams(collective_id=0, has_side_effects=True),
    )(
        low_sino, angle_weight, angle_bias[None], column_weight, column_bias[None], head_weight[None],
        sparse_views, measured, row_weights,
    )


def solution(mesh):
    in_specs = (
        P(("parts", "wide"), None, None, ("narrow", "pair")),
        P(),
        P(),
        P(),
        P(),
        P(),
        P(("parts", "narrow"), None),
        P("parts", "wide", ("narrow", "pair")),
        P(("narrow", "pair"), None),
    )
    out_specs = (P("parts", "wide", ("narrow", "pair")), P("parts", "wide", ("narrow", "pair")))
    body = functools.partial(local, mesh.shape["wide"], mesh.shape["narrow"], mesh.shape["pair"])
    return jax.shard_map(body, mesh=mesh, in_specs=in_specs, out_specs=out_specs, check_vma=False)
```

```python
import functools

import jax
import jax.numpy as jnp
from jax import lax
from jax.experimental import pallas as pl
from jax.experimental.pallas import tpu as pltpu
from jax.sharding import PartitionSpec as P

F32 = jnp.float32
BF16 = jnp.bfloat16


def indices(rows, cols, axis):
    return lax.broadcasted_iota(jnp.int32, (rows, cols), axis).astype(F32)


def div(values, divisor):
    return jnp.floor((values + 0.5) * (1.0 / divisor))


def one_hot(hit):
    return jnp.where(hit, 1.0, 0.0).astype(F32)


def leaky(values):
    return jnp.maximum(values, 0.1 * values)


def nt_dot(left, right, precision=None):
    return lax.dot_general(
        left, right, (((1,), (1,)), ((), ())), precision=precision, preferred_element_type=F32
    )


def angle_matrix(weight, chans):
    size = 4 * chans
    row, col = indices(size, size, 0), indices(size, size, 1)
    row_block, col_block = div(row, chans), div(col, chans)
    spread_row = indices(size, chans, 0)
    left = one_hot(spread_row - chans * div(spread_row, chans) == indices(size, chans, 1)).astype(BF16)
    spread_col = indices(chans, size, 1)
    right = one_hot(spread_col - chans * div(spread_col, chans) == indices(chans, size, 0)).astype(BF16)
    parity, side = div(row_block, 2), div(col_block, 2)
    same = (row_block - 2 * parity) == (col_block - 2 * side)
    total = jnp.zeros((size, size), F32)
    for tap in range(4):
        spread = nt_dot(left, weight[tap]).astype(BF16)
        spread = jnp.dot(spread, right, preferred_element_type=F32)
        total = jnp.where(same & (parity + 2 * side == tap), spread, total)
    return total.astype(BF16)


def column_matrix(weight, chans, outs, first, last):
    rows, cols = chans * outs, 2 * (outs + 1) * chans
    row, col = indices(rows, cols, 0), indices(rows, cols, 1)
    out_col = row - outs * div(row, outs)
    in_col = div(col, chans)
    left = one_hot(div(indices(rows, chans, 0), outs) == indices(rows, chans, 1)).astype(BF16)
    spread_col = indices(chans, cols, 1)
    right = one_hot(spread_col - chans * div(spread_col, chans) == indices(chans, cols, 0)).astype(BF16)
    total = jnp.zeros((rows, cols), F32)
    for tap in range(4):
        spread = nt_dot(left, weight[tap]).astype(BF16)
        spread = jnp.dot(spread, right, preferred_element_type=F32)
        total = jnp.where(in_col - 2 * out_col == tap, spread, total)
    outside = ((in_col == 0) & first) | ((in_col == 2 * outs + 1) & last)
    return jnp.where(outside, 0.0, total).astype(BF16)


def kernel(
    wide, narrow, pair, outs,
    x_hbm, aw_hbm, ab_hbm, cw_hbm, cb_hbm, hw_hbm, sv_hbm, meas_hbm, rw_hbm,
    pred_out, adj_out,
    x_in, x_cols, x_all, aw, ab, cw, cb, hw, sv_all, sv_s, meas_all, rows_m, rw,
    pred_all, picks,
    in_sem, sv_sem, x_send, x_recv, m_send, m_recv, s_send, s_recv, p_send, p_recv,
):
    me = lax.axis_index("wide")
    my_n, my_p = lax.axis_index("narrow"), lax.axis_index("pair")
    group = narrow * pair
    my_g = my_n * pair + my_p
    chans, lanes = x_in.shape[1], x_in.shape[3]
    views = x_in.shape[0]
    pairs = outs + 1
    all_views = wide * views
    keep = meas_all.shape[1]

    def row_peer(step):
        other = lax.rem(my_g + step, group)
        return other, {"narrow": lax.div(other, pair), "pair": lax.rem(other, pair)}

    barrier = pltpu.get_barrier_semaphore()
    for step in range(1, wide):
        pl.semaphore_signal(
            barrier, inc=1, device_id={"wide": lax.rem(me + step, wide)}, device_id_type=pl.DeviceIdType.MESH
        )
    for step in range(1, group):
        pl.semaphore_signal(
            barrier, inc=1, device_id=row_peer(step)[1], device_id_type=pl.DeviceIdType.MESH
        )

    loads = [
        pltpu.make_async_copy(source, target, in_sem.at[spot])
        for spot, (source, target) in enumerate(
            [
                (x_hbm, x_in), (aw_hbm, aw), (ab_hbm, ab), (cw_hbm, cw), (cb_hbm, cb), (hw_hbm, hw),
                (rw_hbm, rw), (meas_hbm, meas_all.at[my_g]), (sv_hbm, sv_all.at[my_n]),
            ]
        )
    ]
    for load in loads:
        load.start()

    loads[0].wait()
    blank = jnp.zeros((1, chans, lanes), F32)
    for view in range(views):
        turned = jnp.swapaxes(x_in[view].astype(F32), 0, 1)
        padded = jnp.concatenate([blank, turned, blank], axis=0)
        x_cols[view] = padded.reshape(x_cols.shape[1], 2 * chans, lanes).astype(BF16)

    pl.semaphore_wait(barrier, wide - 1 + group - 1)

    order = sorted(range(1, wide), key=lambda step: abs(step - wide // 2))
    sends = []
    for step in order:
        target = lax.rem(me + step, wide)
        sends.append(
            pltpu.make_async_remote_copy(
                src_ref=x_cols.at[:, pl.ds(outs * target, pairs)],
                dst_ref=x_all.at[me],
                send_sem=x_send.at[step],
                recv_sem=x_recv.at[me],
                device_id={"wide": target},
                device_id_type=pl.DeviceIdType.MESH,
            )
        )
        sends[-1].start()
    loads[7].wait()
    loads[8].wait()
    for step in range(1, group):
        other, where = row_peer(step)
        sends.append(
            pltpu.make_async_remote_copy(
                src_ref=meas_all.at[my_g],
                dst_ref=meas_all.at[my_g],
                send_sem=m_send.at[step],
                recv_sem=m_recv.at[my_g],
                device_id=where,
                device_id_type=pl.DeviceIdType.MESH,
            )
        )
        sends[-1].start()
    for step in range(1, narrow):
        sends.append(
            pltpu.make_async_remote_copy(
                src_ref=sv_all.at[my_n],
                dst_ref=sv_all.at[my_n],
                send_sem=s_send.at[step],
                recv_sem=s_recv.at[my_n],
                device_id={"narrow": lax.rem(my_n + step, narrow)},
                device_id_type=pl.DeviceIdType.MESH,
            )
        )
        sends[-1].start()
    x_all[me] = x_cols[:, pl.ds(outs * me, pairs)]

    for load in loads[1:7]:
        load.wait()
    angle = angle_matrix(aw, chans)
    column = column_matrix(cw, chans, outs, me == 0, me == wide - 1)
    pick_row = indices(4 * chans, chans, 0)
    angle_bias = jnp.sum(
        one_hot(pick_row - chans * div(pick_row, chans) == indices(4 * chans, chans, 1)) * ab[...],
        axis=1, keepdims=True,
    )
    head_hot = one_hot(div(indices(outs * chans, chans, 0), outs) == indices(outs * chans, chans, 1))
    column_bias = jnp.sum(head_hot * cb[...], axis=1, keepdims=True)
    head = jnp.sum(head_hot * hw[...], axis=1, keepdims=True)

    def wait_for(block, sem):
        pltpu.make_async_remote_copy(
            src_ref=block, dst_ref=block, send_sem=x_send.at[0], recv_sem=sem,
            device_id={"wide": me}, device_id_type=pl.DeviceIdType.MESH,
        ).wait_recv()

    for step in range(1, group):
        other = row_peer(step)[0]
        wait_for(meas_all.at[other], m_recv.at[other])
    for step in range(1, narrow):
        other = lax.rem(my_n + step, narrow)
        wait_for(sv_all.at[other], s_recv.at[other])
    fetch = pltpu.make_async_copy(sv_all, sv_s, sv_sem)
    fetch.start()
    for block in range(group):
        for spot in range(keep):
            rows_m[pl.ds(spot * outs, outs), pl.ds(block * lanes, lanes)] = meas_all[block, spot]
    measured = nt_dot(rows_m[...], rw[...], lax.Precision.HIGHEST)
    rows_m[:, : rw.shape[0]] = measured
    fetch.wait()

    fold = 8 // outs
    arrived = set()
    for step in range(wide):
        for near in (step, step + wide - 1):
            near %= wide
            if near and near not in arrived:
                source = lax.rem(me + near, wide)
                wait_for(x_all.at[source], x_recv.at[source])
                arrived.add(near)
        for view in range(views):
            now = lax.rem(me + step, wide) * views + view
            before = lax.rem(now + all_views - 1, all_views)
            current = x_all[lax.div(now, views), lax.rem(now, views)]
            previous = x_all[lax.div(before, views), lax.rem(before, views)]
            inputs = jnp.concatenate(
                [
                    jnp.concatenate([current[spot], previous[spot]], axis=0)
                    for spot in range(pairs)
                ],
                axis=1,
            )
            raised = jnp.dot(angle, inputs, preferred_element_type=F32)
            raised = leaky(raised + angle_bias).astype(BF16)
            stacked = jnp.concatenate(
                [
                    jnp.concatenate(
                        [
                            raised[parity * 2 * chans : (parity + 1) * 2 * chans, spot * lanes : (spot + 1) * lanes]
                            for spot in range(pairs)
                        ],
                        axis=0,
                    )
                    for parity in range(2)
                ],
                axis=1,
            )
            hidden = jnp.dot(column, stacked, preferred_element_type=F32)
            hidden = leaky(hidden + column_bias) * head
            summed = jnp.sum(hidden.reshape(chans // fold, 8, 2 * lanes), axis=0)
            even, odd = summed[:, :lanes], summed[:, lanes:]
            shift = outs
            while shift < 8:
                even = even + pltpu.roll(even, shift, axis=0)
                odd = odd + pltpu.roll(odd, shift, axis=0)
                shift *= 2
            row = lax.broadcasted_iota(jnp.int32, even.shape, 0)
            both = jnp.where(row < outs, even, odd)
            pred_all[my_g, now] = both
            pred_out[2 * now] = both[:outs]
            pred_out[2 * now + 1] = both[outs : 2 * outs]

    finals = []
    for step in range(1, group):
        other, where = row_peer(step)
        finals.append(
            pltpu.make_async_remote_copy(
                src_ref=pred_all.at[my_g],
                dst_ref=pred_all.at[my_g],
                send_sem=p_send.at[step],
                recv_sem=p_recv.at[my_g],
                device_id=where,
                device_id_type=pl.DeviceIdType.MESH,
            )
        )
        finals[-1].start()
    for step in range(1, group):
        other = row_peer(step)[0]
        wait_for(pred_all.at[other], p_recv.at[other])

    for band in range(narrow):
        total = jnp.zeros((8 * all_views, rw.shape[0]), F32)
        for block in range(band * pair, (band + 1) * pair):
            total += nt_dot(
                pred_all[block].reshape(8 * all_views, lanes),
                rw[:, block * lanes : (block + 1) * lanes],
                lax.Precision.HIGHEST,
            )
        for view in range(all_views):
            picks[band, 2 * view] = total[8 * view : 8 * view + outs]
            picks[band, 2 * view + 1] = total[8 * view + outs : 8 * view + 2 * outs]
    for spot in range(keep):
        value = picks[0, sv_s[0, 0, spot]]
        for band in range(1, narrow):
            value = value + picks[band, sv_s[band, 0, spot]]
        adj_out[spot] = value - rows_m[pl.ds(spot * outs, outs), : rw.shape[0]]
    for send in sends + finals:
        send.wait_send()


def write_out(pred_in, adj_in, pred_hbm, adj_hbm, sems):
    copies = [
        pltpu.make_async_copy(pred_in, pred_hbm, sems.at[0]),
        pltpu.make_async_copy(adj_in, adj_hbm, sems.at[1]),
    ]
    for copy in copies:
        copy.start()
    for copy in copies:
        copy.wait()


def local(
    wide, narrow, pair,
    low_sino, angle_weight, angle_bias, column_weight, column_bias, head_weight,
    sparse_views, measured, row_weights,
):
    views, chans, cols, lanes = low_sino.shape
    keep, outs, _ = measured.shape
    depth = row_weights.shape[0]
    group = narrow * pair
    all_views = wide * views
    any_space = pl.BlockSpec(memory_space=pl.ANY)
    dma = pltpu.SemaphoreType.DMA
    vmem = pl.BlockSpec(memory_space=pltpu.VMEM)
    shapes = ((2 * all_views, outs, lanes), (keep, outs, depth))
    held = pl.pallas_call(
        functools.partial(kernel, wide, narrow, pair, outs),
        out_shape=tuple(pltpu.VMEM(shape, F32) for shape in shapes),
        in_specs=[any_space] * 9,
        out_specs=(vmem, vmem),
        scratch_shapes=[
            pltpu.VMEM(low_sino.shape, BF16),
            pltpu.VMEM((views, cols // 2 + 1, 2 * chans, lanes), BF16),
            pltpu.VMEM((wide, views, outs + 1, 2 * chans, lanes), BF16),
            pltpu.VMEM(angle_weight.shape, BF16),
            pltpu.VMEM((1, chans), F32),
            pltpu.VMEM(column_weight.shape, BF16),
            pltpu.VMEM((1, chans), F32),
            pltpu.VMEM((1, chans), F32),
            pltpu.VMEM((narrow, 1, keep), jnp.int32),
            pltpu.SMEM((narrow, 1, keep), jnp.int32),
            pltpu.VMEM((group, keep, outs, lanes), F32),
            pltpu.VMEM((keep * outs, group * lanes), F32),
            pltpu.VMEM(row_weights.shape, F32),
            pltpu.VMEM((group, all_views, 8, lanes), F32),
            pltpu.VMEM((narrow, 2 * all_views, outs, depth), F32),
            dma((9,)), dma,
            dma((wide,)), dma((wide,)),
            dma((group,)), dma((group,)),
            dma((narrow,)), dma((narrow,)),
            dma((group,)), dma((group,)),
        ],
        compiler_params=pltpu.CompilerParams(collective_id=0, has_side_effects=True),
    )(
        low_sino, angle_weight, angle_bias[None], column_weight, column_bias[None], head_weight[None],
        sparse_views, measured, row_weights,
    )
    return pl.pallas_call(
        write_out,
        out_shape=tuple(jax.ShapeDtypeStruct(shape, F32) for shape in shapes),
        in_specs=[vmem, vmem],
        out_specs=(any_space, any_space),
        scratch_shapes=[dma((2,))],
    )(*(pltpu.with_memory_space_constraint(x, pltpu.VMEM) for x in held))


def solution(mesh):
    in_specs = (
        P(("parts", "wide"), None, None, ("narrow", "pair")),
        P(),
        P(),
        P(),
        P(),
        P(),
        P(("parts", "narrow"), None),
        P("parts", "wide", ("narrow", "pair")),
        P(("narrow", "pair"), None),
    )
    out_specs = (P("parts", "wide", ("narrow", "pair")), P("parts", "wide", ("narrow", "pair")))
    body = functools.partial(local, mesh.shape["wide"], mesh.shape["narrow"], mesh.shape["pair"])
    return jax.shard_map(body, mesh=mesh, in_specs=in_specs, out_specs=out_specs, check_vma=False)
```

```python
import functools

import jax
import jax.numpy as jnp
from jax import lax
from jax.experimental import pallas as pl
from jax.experimental.pallas import tpu as pltpu
from jax.sharding import PartitionSpec as P

F32 = jnp.float32
BF16 = jnp.bfloat16


def indices(rows, cols, axis):
    return lax.broadcasted_iota(jnp.int32, (rows, cols), axis).astype(F32)


def div(values, divisor):
    return jnp.floor((values + 0.5) * (1.0 / divisor))


def one_hot(hit):
    return jnp.where(hit, 1.0, 0.0).astype(F32)


def leaky(values):
    return jnp.maximum(values, 0.1 * values)


def nt_dot(left, right, precision=None):
    return lax.dot_general(
        left, right, (((1,), (1,)), ((), ())), precision=precision, preferred_element_type=F32
    )


def angle_matrix(weight, chans):
    size = 4 * chans
    row, col = indices(size, size, 0), indices(size, size, 1)
    row_block, col_block = div(row, chans), div(col, chans)
    spread_row = indices(size, chans, 0)
    left = one_hot(spread_row - chans * div(spread_row, chans) == indices(size, chans, 1)).astype(BF16)
    spread_col = indices(chans, size, 1)
    right = one_hot(spread_col - chans * div(spread_col, chans) == indices(chans, size, 0)).astype(BF16)
    parity, side = div(row_block, 2), div(col_block, 2)
    same = (row_block - 2 * parity) == (col_block - 2 * side)
    total = jnp.zeros((size, size), F32)
    for tap in range(4):
        spread = nt_dot(left, weight[tap]).astype(BF16)
        spread = jnp.dot(spread, right, preferred_element_type=F32)
        total = jnp.where(same & (parity + 2 * side == tap), spread, total)
    return total.astype(BF16)


def column_matrix(weight, chans, outs, first, last):
    rows, cols = chans * outs, 2 * (outs + 1) * chans
    row, col = indices(rows, cols, 0), indices(rows, cols, 1)
    out_col = row - outs * div(row, outs)
    in_col = div(col, chans)
    left = one_hot(div(indices(rows, chans, 0), outs) == indices(rows, chans, 1)).astype(BF16)
    spread_col = indices(chans, cols, 1)
    right = one_hot(spread_col - chans * div(spread_col, chans) == indices(chans, cols, 0)).astype(BF16)
    total = jnp.zeros((rows, cols), F32)
    for tap in range(4):
        spread = nt_dot(left, weight[tap]).astype(BF16)
        spread = jnp.dot(spread, right, preferred_element_type=F32)
        total = jnp.where(in_col - 2 * out_col == tap, spread, total)
    outside = ((in_col == 0) & first) | ((in_col == 2 * outs + 1) & last)
    return jnp.where(outside, 0.0, total).astype(BF16)


def kernel(
    wide, narrow, pair, outs,
    x_hbm, aw_hbm, ab_hbm, cw_hbm, cb_hbm, hw_hbm, sv_hbm, meas_hbm, rw_hbm,
    pred_out, adj_out,
    x_in, x_cols, x_all, aw, ab, cw, cb, hw, sv_all, sv_s, meas_all, rows_m, rw,
    pred_all, picks,
    in_sem, sv_sem, x_send, x_recv, m_send, m_recv, s_send, s_recv, p_send, p_recv,
):
    me = lax.axis_index("wide")
    my_n, my_p = lax.axis_index("narrow"), lax.axis_index("pair")
    group = narrow * pair
    my_g = my_n * pair + my_p
    chans, lanes = x_in.shape[1], x_in.shape[3]
    views = x_in.shape[0]
    pairs = outs + 1
    all_views = wide * views
    keep = meas_all.shape[1]

    def row_peer(step):
        other = lax.rem(my_g + step, group)
        return other, {"narrow": lax.div(other, pair), "pair": lax.rem(other, pair)}

    barrier = pltpu.get_barrier_semaphore()
    for step in range(1, wide):
        pl.semaphore_signal(
            barrier, inc=1, device_id={"wide": lax.rem(me + step, wide)}, device_id_type=pl.DeviceIdType.MESH
        )
    for step in range(1, group):
        pl.semaphore_signal(
            barrier, inc=1, device_id=row_peer(step)[1], device_id_type=pl.DeviceIdType.MESH
        )

    loads = [
        pltpu.make_async_copy(source, target, in_sem.at[spot])
        for spot, (source, target) in enumerate(
            [
                (x_hbm, x_in), (aw_hbm, aw), (ab_hbm, ab), (cw_hbm, cw), (cb_hbm, cb), (hw_hbm, hw),
                (rw_hbm, rw), (meas_hbm, meas_all.at[my_g]), (sv_hbm, sv_all.at[my_n]),
            ]
        )
    ]
    for load in loads:
        load.start()

    loads[0].wait()
    blank = jnp.zeros((1, chans, lanes), F32)
    for view in range(views):
        turned = jnp.swapaxes(x_in[view].astype(F32), 0, 1)
        padded = jnp.concatenate([blank, turned, blank], axis=0)
        x_cols[view] = padded.reshape(x_cols.shape[1], 2 * chans, lanes).astype(BF16)

    pl.semaphore_wait(barrier, wide - 1 + group - 1)

    order = range(1, wide)
    sends = []
    for step in order:
        target = lax.rem(me + step, wide)
        sends.append(
            pltpu.make_async_remote_copy(
                src_ref=x_cols.at[:, pl.ds(outs * target, pairs)],
                dst_ref=x_all.at[me],
                send_sem=x_send.at[step],
                recv_sem=x_recv.at[me],
                device_id={"wide": target},
                device_id_type=pl.DeviceIdType.MESH,
            )
        )
        sends[-1].start()
    loads[8].wait()
    for step in range(1, narrow):
        sends.append(
            pltpu.make_async_remote_copy(
                src_ref=sv_all.at[my_n],
                dst_ref=sv_all.at[my_n],
                send_sem=s_send.at[step],
                recv_sem=s_recv.at[my_n],
                device_id={"narrow": lax.rem(my_n + step, narrow)},
                device_id_type=pl.DeviceIdType.MESH,
            )
        )
        sends[-1].start()
    loads[7].wait()
    for step in range(1, group):
        other, where = row_peer(step)
        sends.append(
            pltpu.make_async_remote_copy(
                src_ref=meas_all.at[my_g],
                dst_ref=meas_all.at[my_g],
                send_sem=m_send.at[step],
                recv_sem=m_recv.at[my_g],
                device_id=where,
                device_id_type=pl.DeviceIdType.MESH,
            )
        )
        sends[-1].start()
    x_all[me] = x_cols[:, pl.ds(outs * me, pairs)]

    for load in loads[1:7]:
        load.wait()
    angle = angle_matrix(aw, chans)
    column = column_matrix(cw, chans, outs, me == 0, me == wide - 1)
    pick_row = indices(4 * chans, chans, 0)
    angle_bias = jnp.sum(
        one_hot(pick_row - chans * div(pick_row, chans) == indices(4 * chans, chans, 1)) * ab[...],
        axis=1, keepdims=True,
    )
    head_hot = one_hot(div(indices(outs * chans, chans, 0), outs) == indices(outs * chans, chans, 1))
    column_bias = jnp.sum(head_hot * cb[...], axis=1, keepdims=True)
    head = jnp.sum(head_hot * hw[...], axis=1, keepdims=True)

    def wait_for(block, sem):
        pltpu.make_async_remote_copy(
            src_ref=block, dst_ref=block, send_sem=x_send.at[0], recv_sem=sem,
            device_id={"wide": me}, device_id_type=pl.DeviceIdType.MESH,
        ).wait_recv()

    fold = 8 // outs
    arrived = set()
    for step in range(wide):
        for near in (step, step + wide - 1):
            near %= wide
            if near and near not in arrived:
                source = lax.rem(me + near, wide)
                wait_for(x_all.at[source], x_recv.at[source])
                arrived.add(near)
        for view in range(views):
            now = lax.rem(me + step, wide) * views + view
            before = lax.rem(now + all_views - 1, all_views)
            current = x_all[lax.div(now, views), lax.rem(now, views)]
            previous = x_all[lax.div(before, views), lax.rem(before, views)]
            inputs = jnp.concatenate(
                [
                    jnp.concatenate([current[spot], previous[spot]], axis=0)
                    for spot in range(pairs)
                ],
                axis=1,
            )
            raised = jnp.dot(angle, inputs, preferred_element_type=F32)
            raised = leaky(raised + angle_bias).astype(BF16)
            stacked = jnp.concatenate(
                [
                    jnp.concatenate(
                        [
                            raised[parity * 2 * chans : (parity + 1) * 2 * chans, spot * lanes : (spot + 1) * lanes]
                            for spot in range(pairs)
                        ],
                        axis=0,
                    )
                    for parity in range(2)
                ],
                axis=1,
            )
            hidden = jnp.dot(column, stacked, preferred_element_type=F32)
            hidden = leaky(hidden + column_bias) * head
            summed = jnp.sum(hidden.reshape(chans // fold, 8, 2 * lanes), axis=0)
            even, odd = summed[:, :lanes], summed[:, lanes:]
            shift = outs
            while shift < 8:
                even = even + pltpu.roll(even, shift, axis=0)
                odd = odd + pltpu.roll(odd, shift, axis=0)
                shift *= 2
            row = lax.broadcasted_iota(jnp.int32, even.shape, 0)
            both = jnp.where(row < outs, even, odd)
            pred_all[my_g, now] = both
            pred_out[2 * now] = both[:outs]
            pred_out[2 * now + 1] = both[outs : 2 * outs]

    finals = []
    for step in range(1, group):
        other, where = row_peer(step)
        finals.append(
            pltpu.make_async_remote_copy(
                src_ref=pred_all.at[my_g],
                dst_ref=pred_all.at[my_g],
                send_sem=p_send.at[step],
                recv_sem=p_recv.at[my_g],
                device_id=where,
                device_id_type=pl.DeviceIdType.MESH,
            )
        )
        finals[-1].start()
    for step in range(1, group):
        other = row_peer(step)[0]
        wait_for(meas_all.at[other], m_recv.at[other])
    for step in range(1, narrow):
        other = lax.rem(my_n + step, narrow)
        wait_for(sv_all.at[other], s_recv.at[other])
    fetch = pltpu.make_async_copy(sv_all, sv_s, sv_sem)
    fetch.start()
    for block in range(group):
        for spot in range(keep):
            rows_m[pl.ds(spot * outs, outs), pl.ds(block * lanes, lanes)] = meas_all[block, spot]
    measured = nt_dot(rows_m[...], rw[...], lax.Precision.HIGH)
    rows_m[:, : rw.shape[0]] = measured
    fetch.wait()

    for step in range(1, group):
        other = row_peer(step)[0]
        wait_for(pred_all.at[other], p_recv.at[other])

    for band in range(narrow):
        total = jnp.zeros((8 * all_views, rw.shape[0]), F32)
        for block in range(band * pair, (band + 1) * pair):
            total += nt_dot(
                pred_all[block].reshape(8 * all_views, lanes),
                rw[:, block * lanes : (block + 1) * lanes],
                lax.Precision.HIGH,
            )
        for view in range(all_views):
            picks[band, 2 * view] = total[8 * view : 8 * view + outs]
            picks[band, 2 * view + 1] = total[8 * view + outs : 8 * view + 2 * outs]
    for spot in range(keep):
        value = picks[0, sv_s[0, 0, spot]]
        for band in range(1, narrow):
            value = value + picks[band, sv_s[band, 0, spot]]
        adj_out[spot] = value - rows_m[pl.ds(spot * outs, outs), : rw.shape[0]]
    for send in sends + finals:
        send.wait_send()


def write_out(pred_in, adj_in, pred_hbm, adj_hbm, sems):
    copies = [
        pltpu.make_async_copy(pred_in, pred_hbm, sems.at[0]),
        pltpu.make_async_copy(adj_in, adj_hbm, sems.at[1]),
    ]
    for copy in copies:
        copy.start()
    for copy in copies:
        copy.wait()


def local(
    wide, narrow, pair,
    low_sino, angle_weight, angle_bias, column_weight, column_bias, head_weight,
    sparse_views, measured, row_weights,
):
    views, chans, cols, lanes = low_sino.shape
    keep, outs, _ = measured.shape
    depth = row_weights.shape[0]
    group = narrow * pair
    all_views = wide * views
    any_space = pl.BlockSpec(memory_space=pl.ANY)
    dma = pltpu.SemaphoreType.DMA
    vmem = pl.BlockSpec(memory_space=pltpu.VMEM)
    shapes = ((2 * all_views, outs, lanes), (keep, outs, depth))
    held = pl.pallas_call(
        functools.partial(kernel, wide, narrow, pair, outs),
        out_shape=tuple(pltpu.VMEM(shape, F32) for shape in shapes),
        in_specs=[any_space] * 9,
        out_specs=(vmem, vmem),
        scratch_shapes=[
            pltpu.VMEM(low_sino.shape, BF16),
            pltpu.VMEM((views, cols // 2 + 1, 2 * chans, lanes), BF16),
            pltpu.VMEM((wide, views, outs + 1, 2 * chans, lanes), BF16),
            pltpu.VMEM(angle_weight.shape, BF16),
            pltpu.VMEM((1, chans), F32),
            pltpu.VMEM(column_weight.shape, BF16),
            pltpu.VMEM((1, chans), F32),
            pltpu.VMEM((1, chans), F32),
            pltpu.VMEM((narrow, 1, keep), jnp.int32),
            pltpu.SMEM((narrow, 1, keep), jnp.int32),
            pltpu.VMEM((group, keep, outs, lanes), F32),
            pltpu.VMEM((keep * outs, group * lanes), F32),
            pltpu.VMEM(row_weights.shape, F32),
            pltpu.VMEM((group, all_views, 8, lanes), F32),
            pltpu.VMEM((narrow, 2 * all_views, outs, depth), F32),
            dma((9,)), dma,
            dma((wide,)), dma((wide,)),
            dma((group,)), dma((group,)),
            dma((narrow,)), dma((narrow,)),
            dma((group,)), dma((group,)),
        ],
        compiler_params=pltpu.CompilerParams(collective_id=0, has_side_effects=True),
    )(
        low_sino, angle_weight, angle_bias[None], column_weight, column_bias[None], head_weight[None],
        sparse_views, measured, row_weights,
    )
    return pl.pallas_call(
        write_out,
        out_shape=tuple(jax.ShapeDtypeStruct(shape, F32) for shape in shapes),
        in_specs=[vmem, vmem],
        out_specs=(any_space, any_space),
        scratch_shapes=[dma((2,))],
    )(*(pltpu.with_memory_space_constraint(x, pltpu.VMEM) for x in held))


def solution(mesh):
    in_specs = (
        P(("parts", "wide"), None, None, ("narrow", "pair")),
        P(),
        P(),
        P(),
        P(),
        P(),
        P(("parts", "narrow"), None),
        P("parts", "wide", ("narrow", "pair")),
        P(("narrow", "pair"), None),
    )
    out_specs = (P("parts", "wide", ("narrow", "pair")), P("parts", "wide", ("narrow", "pair")))
    body = functools.partial(local, mesh.shape["wide"], mesh.shape["narrow"], mesh.shape["pair"])
    return jax.shard_map(body, mesh=mesh, in_specs=in_specs, out_specs=out_specs, check_vma=False)
```
